32 devices in a mesh: slab: 2 (over x), clus: 16 (over z, y, core).
Axes of the slice: x: 2, y: 2, z: 4, core: 2. Of those that a mesh axis runs over, the one named last changes fastest.
Arguments:
- emb: bfloat16 [8192, 1024], P(('slab', 'clus')), parts along dimension 0, may hold values from -4000 to 4000
- wanted: int32 [512], P(('slab', 'clus')), parts along dimension 0, may hold values from 0 to 31, as said below
- counts: int32 [64], P('slab'), parts along dimension 0, may hold values from 2 to 128, as said below
Outputs:
- best: float32 [16, 8192], P(None, ('slab', 'clus')), parts along dimension 1
- own: float32 [8192], P(('slab', 'clus')), parts along dimension 0
The draws below stay inside these ranges and needn't reach their ends.
There are 2 independent parts, one for each index of `slab`. The reference program is written for one: setup_inputs(seed, part) draws one part's arguments, and reference() takes and returns one part's arrays. A program takes and returns all parts, laid end to end along the dimension named above; each array names one. Nothing has to cross between parts.
Inputs may be any that keep to these rules, and one draw needn't show every extreme that they name: `wanted`: the 16 entries of one group name exactly one cluster of every group (group = cluster // 2), one entry per group. `counts`: some cluster has exactly 128 live rows.
All inputs are finite; a program needn't handle non-finite values.
Results may differ from the reference program's by a relative error of at most 0.0015.
Values may be sent and summed in bfloat16 or wider, within the bound.
A program may use at most 128 MiB of HBM per device.

```python
import math
import jax
import jax.numpy as jnp
from jax import lax

D = 1024
TILE = 128
CL_DEV = 2
CAP = 1
REQ = 16
CLUSTERS = 32
ROWS = 4096
N_CLUS = 16


def wanted_table(key):
    peers = N_CLUS

    def one_group(group_key):
        key_order, key_first, key_second = jax.random.split(group_key, 3)
        slot_peer = (jnp.arange(REQ) // CAP)[jax.random.permutation(key_order, REQ)]
        first = jax.random.randint(key_first, (REQ,), 0, CL_DEV)
        second = jax.random.randint(key_second, (REQ,), 0, CL_DEV)
        return slot_peer * CL_DEV + jnp.minimum(first, second)
    group_keys = jax.random.split(key, peers)
    return jax.vmap(one_group)(group_keys).reshape(-1).astype(jnp.int32)


def counts_table(key):
    key_vals, key_spot = jax.random.split(key, 2)
    values = jax.random.randint(key_vals, (CLUSTERS,), 2, TILE + 1)
    spot = jax.random.randint(key_spot, (), 0, CLUSTERS)
    return values.at[spot].set(TILE).astype(jnp.int32)


def draw_wanted(key, part):
    return wanted_table(jax.random.fold_in(key, 11))


def draw_counts(key, part):
    return counts_table(jax.random.fold_in(key, 12))


def draw_emb(key, part):
    wanted = wanted_table(jax.random.fold_in(key, 11))
    counts = counts_table(jax.random.fold_in(key, 12))
    keys = jax.random.split(jax.random.fold_in(key, 13), 7)
    base = jax.random.normal(keys[0], (ROWS, D), jnp.float32)
    group = jnp.arange(ROWS) // (CL_DEV * TILE)
    pick = jax.random.randint(keys[1], (ROWS,), 0, REQ)
    target = wanted[group * REQ + pick]
    offset = jax.random.randint(keys[2], (ROWS,), 0, counts[target])
    source = target * TILE + offset
    mixing = jax.random.uniform(keys[3], (ROWS,), jnp.float32, 0.5, 2.0)
    mixing = mixing * jax.random.randint(keys[4], (ROWS,), 0, 2).astype(jnp.float32)
    row_scale = jnp.exp(jax.random.uniform(keys[5], (ROWS,), jnp.float32, 0.0, math.log(10.0)))
    col_scale = jnp.exp(jax.random.uniform(keys[6], (D,), jnp.float32, 0.0, math.log(10.0)))
    values = (base + mixing[:, None] * base[source]) * row_scale[:, None] * col_scale[None, :]
    return values.astype(jnp.bfloat16)


def setup_inputs(seed: int = 0, part: int = 0) -> dict:
    key_of = jax.random.split(jax.random.key(seed), 4)
    part_keys = jax.random.split(jax.random.fold_in(key_of[3], part), 4)
    return {
        "emb": draw_emb(jax.random.fold_in(jax.random.fold_in(key_of[3], part), 71), part),
        "wanted": draw_wanted(jax.random.fold_in(jax.random.fold_in(key_of[3], part), 71), part),
        "counts": draw_counts(jax.random.fold_in(jax.random.fold_in(key_of[3], part), 71), part),
    }


def unit_rows(values):
    wide = values.astype(jnp.float32)
    total = lax.optimization_barrier(jnp.sum(wide * wide, axis=-1, keepdims=True))
    return (wide * lax.rsqrt(total + 1e-06)).astype(jnp.bfloat16)

def reference(emb, wanted, counts):
    unit = unit_rows(emb)
    blocks = unit.reshape(CLUSTERS, TILE, D)
    rows_dev = CL_DEV * TILE
    index = jnp.arange(TILE, dtype=jnp.int32)

    def per_group(group):
        rows = lax.dynamic_slice_in_dim(unit, group * rows_dev, rows_dev, 0)
        targets = lax.dynamic_slice_in_dim(wanted, group * REQ, REQ, 0)
        tiles = jnp.take(blocks, targets, axis=0).reshape(REQ * TILE, D)
        target_counts = jnp.take(counts, targets)
        product = jnp.dot(rows, tiles.T, preferred_element_type=jnp.float32)
        live_cols = (index[None, :] < target_counts[:, None]).reshape(1, REQ * TILE)
        product = jnp.where(live_cols, product, -jnp.inf)
        best_part = lax.optimization_barrier(jnp.max(product.reshape(rows_dev, REQ, TILE), axis=2)).T
        own_counts = lax.dynamic_slice_in_dim(counts, group * CL_DEV, CL_DEV, 0)
        row_live = (index[None, :] < own_counts[:, None]).reshape(rows_dev)
        local_blocks = rows.reshape(CL_DEV, TILE, D).astype(jnp.float32)
        inner = jnp.einsum('bid,bjd->bij', local_blocks, local_blocks)
        keep = (index[None, None, :] < own_counts[:, None, None]) & (index[:, None] != index[None, :])[None]
        own_part = lax.optimization_barrier(jnp.max(jnp.where(keep, inner, -jnp.inf), axis=2)).reshape(rows_dev)
        best_part = jnp.where(row_live[None, :], best_part, 0.0)
        own_part = jnp.where(row_live, own_part, 0.0)
        return (best_part, own_part)
    best_all, own_all = lax.map(per_group, jnp.arange(N_CLUS, dtype=jnp.int32))
    best = jnp.transpose(best_all, (1, 0, 2)).reshape(REQ, ROWS)
    return (best, own_all.reshape(ROWS))
```

```python
import functools
import jax
import jax.numpy as jnp
from jax import lax
from jax.experimental import pallas as pl
from jax.experimental.pallas import tpu as pltpu
from jax.sharding import PartitionSpec as P

TILE = 128
CORES = 2
LAYER = 4
MESH = pl.DeviceIdType.MESH
NT = (((1,), (1,)), ((), ()))


def ring(chips, cols):
    def chip_at(pos):
        pos = lax.rem(pos + 4 * chips, chips)
        if cols == 1:
            return pos
        back = pos // (chips // 2)
        return (pos + back * (chips - 1 - 2 * pos)) * 2 + back

    def pos_of(chip):
        if cols == 1:
            return chip
        z, y = chip // 2, lax.rem(chip, 2)
        return z + y * (chips - 1 - 2 * z)

    return chip_at, pos_of


def kernel(
    chips, cols, wanted_ref, counts_ref, emb_ref, best_ref, own_ref,
    unit, from_l, from_r, across, table, res_a, res_b,
    r_send, r_recv, l_send, l_recv, x_send, x_recv,
    a_send, a_recv, b_send, b_recv,
):
    rows, width = emb_ref.shape
    parts = rows // TILE
    reach = chips // 4
    far = 2 * reach
    chip_at, pos_of = ring(chips, cols)
    me = lax.axis_index("clus")
    core = lax.rem(me, CORES)
    other = 1 - core
    pos = pos_of(me // CORES)

    def dev(p, c):
        return chip_at(p) * CORES + c

    def crossed(p):
        return lax.rem(p + 4 * chips, chips) // (chips // 2)

    def swap(p, c):
        x = crossed(p)
        return c + x * (1 - 2 * c)

    barrier = pltpu.get_barrier_semaphore()

    def greet(target):
        pl.semaphore_signal(barrier, inc=1, device_id={"clus": target}, device_id_type=MESH)

    greet(dev(pos, other))
    for i in range(1, reach + 1):
        greet(dev(pos + i, core))
    for j in range(1, reach):
        greet(dev(pos - j, 0))
        greet(dev(pos - j, 1))
    greet(dev(pos - reach, swap(pos - reach, core)))

    @pl.when(crossed(pos) == 1)
    def _():
        greet(dev(pos + 1, other))

    def remote(src, dst, send, recv, target):
        return pltpu.make_async_remote_copy(
            src_ref=src, dst_ref=dst, send_sem=send, recv_sem=recv,
            device_id={"clus": target}, device_id_type=MESH,
        )

    def right(h, q):
        src = unit if h == 0 else from_l.at[h - 1]
        return remote(src.at[q], from_l.at[h, q], r_send.at[h, q], r_recv.at[h, q], dev(pos + 1, core))

    def left(h, q):
        src = unit if h == 0 else from_r.at[h - 1]
        c = swap(pos - 1, core) if h == reach - 1 else core
        return remote(src.at[q], from_r.at[h, q], l_send.at[h, q], l_recv.at[h, q], dev(pos - 1, c))

    def cross(h, q):
        src = unit if h == 0 else from_r.at[h - 1]
        return remote(src.at[q], across.at[h, q], x_send.at[h, q], x_recv.at[h, q], dev(pos, other))

    def normalize(q):
        step = 32
        for s in range(0, TILE, step):
            wide = emb_ref[q * TILE + s : q * TILE + s + step, :].astype(jnp.float32)
            total = jnp.sum(wide * wide, axis=1, keepdims=True)
            unit[q, s : s + step, :] = (wide * lax.rsqrt(total + 1e-06)).astype(jnp.bfloat16)

    for q in range(parts):
        normalize(q)
        if q == 0:
            pl.semaphore_wait(barrier, 3 * reach + crossed(pos - 1))
        right(0, q).start()
        left(0, q).start()
        cross(0, q).start()

    def rows_of(ref, q):
        return ref[q]

    def product(x, y):
        return lax.dot_general(x, y, NT, preferred_element_type=jnp.float32)

    def top(prod, cluster):
        index = lax.broadcasted_iota(jnp.int32, prod.shape, 0)
        live = index < counts_ref[cluster]
        return jnp.max(jnp.where(live, prod, -jnp.inf), axis=0, keepdims=True)

    def block(ref):
        return ref[...].reshape(parts * TILE, width)

    self_prod = product(block(unit), block(unit))
    for t in range(parts):
        piece = self_prod[t * TILE : (t + 1) * TILE]
        table[me * parts + t] = top(piece, me * parts + t)
        square = piece[:, t * TILE : (t + 1) * TILE]
        i0 = lax.broadcasted_iota(jnp.int32, square.shape, 0)
        i1 = lax.broadcasted_iota(jnp.int32, square.shape, 1)
        count = counts_ref[me * parts + t]
        keep = (i0 < count) & (i0 != i1)
        value = jnp.max(jnp.where(keep, square, -jnp.inf), axis=0, keepdims=True)
        lane = lax.broadcasted_iota(jnp.int32, value.shape, 1)
        own_ref[:, t * TILE : (t + 1) * TILE] = jnp.where(lane < count, value, 0.0)

    for q in range(parts):
        cross(0, q).wait_recv()
    mate = dev(pos, other)
    mate_prod = product(block(across.at[0]), block(unit))
    for t in range(parts):
        table[mate * parts + t] = top(mate_prod[t * TILE : (t + 1) * TILE], mate * parts + t)

    def split(d):
        j = max(1, d // 2)
        return d - j, j

    def a_msg(d):
        i, j = split(d)
        if d == far:
            b = dev(pos + j, swap(pos, core))
            count = parts
        else:
            b = dev(pos + j, 0)
            count = parts * CORES
        return remote(
            res_a.at[d - 1, pl.ds(0, count)], table.at[pl.ds(b * parts, count)],
            a_send.at[d - 1], a_recv.at[d - 1], dev(pos - i, core),
        )

    def b_msg(d, e, slot):
        i, j = split(d)
        target = dev(pos + j, swap(pos, core) if d == far else e)
        a = dev(pos - i, core)
        return remote(
            res_b.at[d - 1, e], table.at[pl.ds(a * parts, parts)],
            b_send.at[d - 1, e], b_recv.at[d - 1, slot], target,
        )

    def messages(d):
        i, _ = split(d)
        found = [b_msg(d, e, 0 if d == far else core) for e in range(1 if d == far else CORES)]
        if i > 0:
            found.append(a_msg(d))
        return found

    def score(d, a_ref, b_ref, e, b_dev, a_q, b_q):
        i, _ = split(d)
        a_dev = dev(pos - i, core)
        qa, qb = a_q, b_q
        a = jnp.concatenate([a_ref[q] for q in qa], axis=0) if len(qa) > 1 else a_ref[qa[0]]
        b = jnp.concatenate([b_ref[q] for q in qb], axis=0) if len(qb) > 1 else b_ref[qb[0]]
        up = product(b, a)
        for n, t in enumerate(qb):
            value = top(up[n * TILE : (n + 1) * TILE], b_dev * parts + t)
            lanes = slice(qa[0] * TILE, (qa[-1] + 1) * TILE)
            if i == 0:
                table[b_dev * parts + t, :, lanes] = value
            else:
                slot = t if d == far else e * parts + t
                res_a[d - 1, slot, :, lanes] = value
        down = product(a, b)
        for n, t in enumerate(qa):
            value = top(down[n * TILE : (n + 1) * TILE], a_dev * parts + t)
            res_b[d - 1, 0 if d == far else e, t, :, qb[0] * TILE : (qb[-1] + 1) * TILE] = value

    every = list(range(parts))

    def near(d, a_q):
        i, j = split(d)
        a_ref = unit if i == 0 else from_l.at[i - 1]
        for mine in (True, False):
            b_ref = from_r.at[j - 1] if mine else across.at[j]
            e = core if mine else other
            score(d, a_ref, b_ref, e, dev(pos + j, e), a_q, every)

    for h in range(1, reach + 1):
        last = h == reach
        for q in range(parts):
            right(h - 1, q).wait_recv()
            if not last:
                right(h, q).start()
            left(h - 1, q).wait_recv()
            if not last:
                left(h, q).start()
                cross(h, q).start()
            if last:
                near(2 * h - 1, [q])
                if q == parts - 1:
                    for msg in messages(2 * h - 1):
                        msg.start()
                b_dev = dev(pos + reach, swap(pos, core))
                pieces = [(q, [z for z in every if z <= q])] + [(z, [q]) for z in range(q)]
                for qa, qb in pieces:
                    score(far, from_l.at[h - 1], from_r.at[h - 1], 0, b_dev, [qa], qb)
        if last:
            for msg in messages(far):
                msg.start()
        else:
            for q in range(parts):
                cross(h, q).wait_recv()
            for d in (2 * h - 1, 2 * h):
                near(d, every)
                for msg in messages(d):
                    msg.start()

    for h in range(reach):
        for q in range(parts):
            right(h, q).wait_send()
            left(h, q).wait_send()
            cross(h, q).wait_send()
    for d in range(1, far + 1):
        for msg in messages(d):
            msg.wait_send()
        for e in range(1 if d == far else CORES):
            b_msg(d, e, e).wait_recv()
        if split(d)[0] > 0:
            a_msg(d).wait_recv()

    lane = lax.broadcasted_iota(jnp.int32, (1, rows), 1)
    live = lane < 0
    for t in range(parts):
        live = live | ((lane >= t * TILE) & (lane < t * TILE + counts_ref[me * parts + t]))
    for k in range(best_ref.shape[0]):
        best_ref[k : k + 1, :] = jnp.where(live, table[wanted_ref[k]], 0.0)


def body(chips, cols, emb, wanted, counts):
    rows, width = emb.shape
    parts = rows // TILE
    reach = chips // 4
    far = 2 * reach
    data = pltpu.SemaphoreType.DMA((reach, parts))
    req = wanted.shape[0]
    smem = pl.BlockSpec(memory_space=pltpu.SMEM)
    vmem = pl.BlockSpec(memory_space=pltpu.VMEM)
    best, own = pl.pallas_call(
        functools.partial(kernel, chips, cols),
        out_shape=(
            jax.ShapeDtypeStruct((req, rows), jnp.float32),
            jax.ShapeDtypeStruct((1, rows), jnp.float32),
        ),
        in_specs=[smem, smem, vmem],
        out_specs=(vmem, vmem),
        scratch_shapes=[
            pltpu.VMEM((parts, TILE, width), jnp.bfloat16),
            pltpu.VMEM((reach, parts, TILE, width), jnp.bfloat16),
            pltpu.VMEM((reach, parts, TILE, width), jnp.bfloat16),
            pltpu.VMEM((reach, parts, TILE, width), jnp.bfloat16),
            pltpu.VMEM((chips * CORES * parts, 1, rows), jnp.float32),
            pltpu.VMEM((far, CORES * parts, 1, rows), jnp.float32),
            pltpu.VMEM((far, CORES, parts, 1, rows), jnp.float32),
            data, data, data, data, data, data,
            pltpu.SemaphoreType.DMA((far,)),
            pltpu.SemaphoreType.DMA((far,)),
            pltpu.SemaphoreType.DMA((far, CORES)),
            pltpu.SemaphoreType.DMA((far, CORES)),
        ],
        compiler_params=pltpu.CompilerParams(collective_id=0, has_side_effects=True),
    )(wanted, counts, emb)
    return best, own.reshape(rows)


def solution(mesh):
    chips = mesh.shape["clus"] // CORES
    cols = LAYER // mesh.shape["slab"]
    in_specs = (P(("slab", "clus"), None), P(("slab", "clus")), P("slab"))
    out_specs = (P(None, ("slab", "clus")), P(("slab", "clus")))
    return jax.shard_map(
        functools.partial(body, chips, cols), mesh=mesh,
        in_specs=in_specs, out_specs=out_specs, check_vma=False,
    )
```

```python
import functools
import jax
import jax.numpy as jnp
from jax import lax
from jax.experimental import pallas as pl
from jax.experimental.pallas import tpu as pltpu
from jax.sharding import PartitionSpec as P

TILE = 128
CORES = 2
LAYER = 4
MESH = pl.DeviceIdType.MESH
NT = (((1,), (1,)), ((), ()))


def ring(chips, cols):
    def chip_at(pos):
        pos = lax.rem(pos + 4 * chips, chips)
        if cols == 1:
            return pos
        back = pos // (chips // 2)
        return (pos + back * (chips - 1 - 2 * pos)) * 2 + back

    def pos_of(chip):
        if cols == 1:
            return chip
        z, y = chip // 2, lax.rem(chip, 2)
        return z + y * (chips - 1 - 2 * z)

    return chip_at, pos_of


def kernel(
    chips, cols, wanted_hbm, counts_hbm, emb_hbm, best_ref, own_ref,
    wanted_ref, counts_ref, emb_ref, load_sem, unit, from_l, from_r, across, table, res_a, res_b,
    r_send, r_recv, l_send, l_recv, x_send, x_recv,
    a_send, a_recv, b_send, b_recv,
):
    rows, width = emb_hbm.shape
    parts = rows // TILE
    reach = chips // 4
    far = 2 * reach
    chip_at, pos_of = ring(chips, cols)
    me = lax.axis_index("clus")
    core = lax.rem(me, CORES)
    other = 1 - core
    pos = pos_of(me // CORES)

    def dev(p, c):
        return chip_at(p) * CORES + c

    def crossed(p):
        return lax.rem(p + 4 * chips, chips) // (chips // 2)

    def swap(p, c):
        x = crossed(p)
        return c + x * (1 - 2 * c)

    barrier = pltpu.get_barrier_semaphore()
    loads = [
        pltpu.make_async_copy(emb_hbm.at[pl.ds(q * TILE, TILE)], emb_ref.at[pl.ds(q * TILE, TILE)], load_sem.at[q])
        for q in range(parts)
    ]
    loads.append(pltpu.make_async_copy(counts_hbm, counts_ref, load_sem.at[parts]))
    loads.append(pltpu.make_async_copy(wanted_hbm, wanted_ref, load_sem.at[parts + 1]))
    for load in loads:
        load.start()

    def greet(target):
        pl.semaphore_signal(barrier, inc=1, device_id={"clus": target}, device_id_type=MESH)

    greet(dev(pos, other))
    greet(dev(pos + 1, core))
    greet(dev(pos - 1, core))

    @pl.when(crossed(pos) == 1)
    def _():
        greet(dev(pos + 1, other))

    def remote(src, dst, send, recv, target):
        return pltpu.make_async_remote_copy(
            src_ref=src, dst_ref=dst, send_sem=send, recv_sem=recv,
            device_id={"clus": target}, device_id_type=MESH,
        )

    def right(h, q):
        src = unit if h == 0 else from_l.at[h - 1]
        return remote(src.at[q], from_l.at[h, q], r_send.at[h, q], r_recv.at[h, q], dev(pos + 1, core))

    def left(h, q):
        src = unit if h == 0 else from_r.at[h - 1]
        c = swap(pos - 1, core) if h == reach - 1 else core
        return remote(src.at[q], from_r.at[h, q], l_send.at[h, q], l_recv.at[h, q], dev(pos - 1, c))

    def cross(h, q):
        src = unit if h == 0 else from_r.at[h - 1]
        return remote(src.at[q], across.at[h, q], x_send.at[h, q], x_recv.at[h, q], dev(pos, other))

    def normalize(q):
        step = 32
        for s in range(0, TILE, step):
            wide = emb_ref[q * TILE + s : q * TILE + s + step, :].astype(jnp.float32)
            total = jnp.sum(wide * wide, axis=1, keepdims=True)
            unit[q, s : s + step, :] = (wide * lax.rsqrt(total + 1e-06)).astype(jnp.bfloat16)

    for q in range(parts):
        loads[q].wait()
        normalize(q)
        if q == 0:
            pl.semaphore_wait(barrier, 3 + crossed(pos - 1))
        right(0, q).start()
        left(0, q).start()
        cross(0, q).start()
    for load in loads[parts:]:
        load.wait()

    def rows_of(ref, q):
        return ref[q]

    def product(x, y):
        return lax.dot_general(x, y, NT, preferred_element_type=jnp.float32)

    def top(prod, cluster):
        index = lax.broadcasted_iota(jnp.int32, prod.shape, 0)
        live = index < counts_ref[cluster]
        return jnp.max(jnp.where(live, prod, -jnp.inf), axis=0, keepdims=True)

    def block(ref):
        return ref[...].reshape(parts * TILE, width)

    self_prod = product(block(unit), block(unit))
    for t in range(parts):
        piece = self_prod[t * TILE : (t + 1) * TILE]
        table[me * parts + t] = top(piece, me * parts + t)
        square = piece[:, t * TILE : (t + 1) * TILE]
        i0 = lax.broadcasted_iota(jnp.int32, square.shape, 0)
        i1 = lax.broadcasted_iota(jnp.int32, square.shape, 1)
        count = counts_ref[me * parts + t]
        keep = (i0 < count) & (i0 != i1)
        value = jnp.max(jnp.where(keep, square, -jnp.inf), axis=0, keepdims=True)
        lane = lax.broadcasted_iota(jnp.int32, value.shape, 1)
        own_ref[:, t * TILE : (t + 1) * TILE] = jnp.where(lane < count, value, 0.0)

    for q in range(parts):
        cross(0, q).wait_recv()
    mate = dev(pos, other)
    mate_prod = product(block(across.at[0]), block(unit))
    for t in range(parts):
        table[mate * parts + t] = top(mate_prod[t * TILE : (t + 1) * TILE], mate * parts + t)

    def split(d):
        j = max(1, d // 2)
        return d - j, j

    def a_msg(d):
        i, j = split(d)
        if d == far:
            b = dev(pos + j, swap(pos, core))
            count = parts
        else:
            b = dev(pos + j, 0)
            count = parts * CORES
        return remote(
            res_a.at[d - 1, pl.ds(0, count)], table.at[pl.ds(b * parts, count)],
            a_send.at[d - 1], a_recv.at[d - 1], dev(pos - i, core),
        )

    def b_msg(d, e, slot):
        i, j = split(d)
        target = dev(pos + j, swap(pos, core) if d == far else e)
        a = dev(pos - i, core)
        return remote(
            res_b.at[d - 1, e], table.at[pl.ds(a * parts, parts)],
            b_send.at[d - 1, e], b_recv.at[d - 1, slot], target,
        )

    def messages(d):
        i, _ = split(d)
        found = [b_msg(d, e, 0 if d == far else core) for e in range(1 if d == far else CORES)]
        if i > 0:
            found.append(a_msg(d))
        return found

    def score(d, a_ref, b_ref, e, b_dev, a_q, b_q):
        i, _ = split(d)
        a_dev = dev(pos - i, core)
        qa, qb = a_q, b_q
        a = jnp.concatenate([a_ref[q] for q in qa], axis=0) if len(qa) > 1 else a_ref[qa[0]]
        b = jnp.concatenate([b_ref[q] for q in qb], axis=0) if len(qb) > 1 else b_ref[qb[0]]
        up = product(b, a)
        for n, t in enumerate(qb):
            value = top(up[n * TILE : (n + 1) * TILE], b_dev * parts + t)
            lanes = slice(qa[0] * TILE, (qa[-1] + 1) * TILE)
            if i == 0:
                table[b_dev * parts + t, :, lanes] = value
            else:
                slot = t if d == far else e * parts + t
                res_a[d - 1, slot, :, lanes] = value
        down = product(a, b)
        for n, t in enumerate(qa):
            value = top(down[n * TILE : (n + 1) * TILE], a_dev * parts + t)
            res_b[d - 1, 0 if d == far else e, t, :, qb[0] * TILE : (qb[-1] + 1) * TILE] = value

    every = list(range(parts))

    def near(d, a_q):
        i, j = split(d)
        a_ref = unit if i == 0 else from_l.at[i - 1]
        for mine in (True, False):
            b_ref = from_r.at[j - 1] if mine else across.at[j]
            e = core if mine else other
            score(d, a_ref, b_ref, e, dev(pos + j, e), a_q, every)

    for h in range(1, reach + 1):
        last = h == reach
        for q in range(parts):
            right(h - 1, q).wait_recv()
            if not last:
                right(h, q).start()
            left(h - 1, q).wait_recv()
            if not last:
                left(h, q).start()
                cross(h, q).start()
            if last:
                near(2 * h - 1, [q])
                if q == parts - 1:
                    for msg in messages(2 * h - 1):
                        msg.start()
                b_dev = dev(pos + reach, swap(pos, core))
                pieces = [(q, [z for z in every if z <= q])] + [(z, [q]) for z in range(q)]
                for qa, qb in pieces:
                    score(far, from_l.at[h - 1], from_r.at[h - 1], 0, b_dev, [qa], qb)
        if last:
            for msg in messages(far):
                msg.start()
        else:
            for q in range(parts):
                cross(h, q).wait_recv()
            for d in (2 * h - 1, 2 * h):
                near(d, every)
                for msg in messages(d):
                    msg.start()

    for h in range(reach):
        for q in range(parts):
            right(h, q).wait_send()
            left(h, q).wait_send()
            cross(h, q).wait_send()
    for d in range(1, far + 1):
        for msg in messages(d):
            msg.wait_send()
        for e in range(1 if d == far else CORES):
            b_msg(d, e, e).wait_recv()
        if split(d)[0] > 0:
            a_msg(d).wait_recv()

    lane = lax.broadcasted_iota(jnp.int32, (1, rows), 1)
    live = lane < 0
    for t in range(parts):
        live = live | ((lane >= t * TILE) & (lane < t * TILE + counts_ref[me * parts + t]))
    for k in range(best_ref.shape[0]):
        best_ref[k : k + 1, :] = jnp.where(live, table[wanted_ref[k]], 0.0)


def body(chips, cols, emb, wanted, counts):
    rows, width = emb.shape
    parts = rows // TILE
    reach = chips // 4
    far = 2 * reach
    data = pltpu.SemaphoreType.DMA((reach, parts))
    req = wanted.shape[0]
    hbm = pl.BlockSpec(memory_space=pltpu.HBM)
    vmem = pl.BlockSpec(memory_space=pltpu.VMEM)
    best, own = pl.pallas_call(
        functools.partial(kernel, chips, cols),
        out_shape=(
            jax.ShapeDtypeStruct((req, rows), jnp.float32),
            jax.ShapeDtypeStruct((1, rows), jnp.float32),
        ),
        in_specs=[hbm, hbm, hbm],
        out_specs=(vmem, vmem),
        scratch_shapes=[
            pltpu.SMEM(wanted.shape, jnp.int32),
            pltpu.SMEM(counts.shape, jnp.int32),
            pltpu.VMEM((rows, width), jnp.bfloat16),
            pltpu.SemaphoreType.DMA((parts + 2,)),
            pltpu.VMEM((parts, TILE, width), jnp.bfloat16),
            pltpu.VMEM((reach, parts, TILE, width), jnp.bfloat16),
            pltpu.VMEM((reach, parts, TILE, width), jnp.bfloat16),
            pltpu.VMEM((reach, parts, TILE, width), jnp.bfloat16),
            pltpu.VMEM((chips * CORES * parts, 1, rows), jnp.float32),
            pltpu.VMEM((far, CORES * parts, 1, rows), jnp.float32),
            pltpu.VMEM((far, CORES, parts, 1, rows), jnp.float32),
            data, data, data, data, data, data,
            pltpu.SemaphoreType.DMA((far,)),
            pltpu.SemaphoreType.DMA((far,)),
            pltpu.SemaphoreType.DMA((far, CORES)),
            pltpu.SemaphoreType.DMA((far, CORES)),
        ],
        compiler_params=pltpu.CompilerParams(collective_id=0, has_side_effects=True),
    )(wanted, counts, emb)
    return best, own.reshape(rows)


def solution(mesh):
    chips = mesh.shape["clus"] // CORES
    cols = LAYER // mesh.shape["slab"]
    in_specs = (P(("slab", "clus"), None), P(("slab", "clus")), P("slab"))
    out_specs = (P(None, ("slab", "clus")), P(("slab", "clus")))
    return jax.shard_map(
        functools.partial(body, chips, cols), mesh=mesh,
        in_specs=in_specs, out_specs=out_specs, check_vma=False,
    )
```

```python
import functools
import jax
import jax.numpy as jnp
from jax import lax
from jax.experimental import pallas as pl
from jax.experimental.pallas import tpu as pltpu
from jax.sharding import PartitionSpec as P

TILE = 128
CORES = 2
LAYER = 4
MESH = pl.DeviceIdType.MESH
NT = (((1,), (1,)), ((), ()))


def ring(chips, cols):
    def chip_at(pos):
        pos = lax.rem(pos + 4 * chips, chips)
        if cols == 1:
            return pos
        back = pos // (chips // 2)
        return (pos + back * (chips - 1 - 2 * pos)) * 2 + back

    def pos_of(chip):
        if cols == 1:
            return chip
        z, y = chip // 2, lax.rem(chip, 2)
        return z + y * (chips - 1 - 2 * z)

    return chip_at, pos_of


def kernel(
    chips, cols, wanted_hbm, counts_hbm, emb_hbm, best_ref, own_ref,
    wanted_ref, counts_ref, emb_ref, load_sem, unit, from_l, from_r, across, table, res_a, res_b,
    r_send, r_recv, l_send, l_recv, x_send, x_recv,
    a_send, a_recv, b_send, b_recv,
):
    rows, width = emb_hbm.shape
    parts = rows // TILE
    reach = chips // 4
    far = 2 * reach
    chip_at, pos_of = ring(chips, cols)
    me = lax.axis_index("clus")
    core = lax.rem(me, CORES)
    other = 1 - core
    pos = pos_of(me // CORES)

    def dev(p, c):
        return chip_at(p) * CORES + c

    def crossed(p):
        return lax.rem(p + 4 * chips, chips) // (chips // 2)

    def swap(p, c):
        x = crossed(p)
        return c + x * (1 - 2 * c)

    barrier = pltpu.get_barrier_semaphore()
    loads = [
        pltpu.make_async_copy(emb_hbm.at[pl.ds(q * TILE, TILE)], emb_ref.at[pl.ds(q * TILE, TILE)], load_sem.at[q])
        for q in range(parts)
    ]
    loads.append(pltpu.make_async_copy(counts_hbm, counts_ref, load_sem.at[parts]))
    loads.append(pltpu.make_async_copy(wanted_hbm, wanted_ref, load_sem.at[parts + 1]))
    for load in loads:
        load.start()

    def greet(target):
        pl.semaphore_signal(barrier, inc=1, device_id={"clus": target}, device_id_type=MESH)

    greet(dev(pos, other))
    greet(dev(pos + 1, core))
    greet(dev(pos - 1, core))

    @pl.when(crossed(pos) == 1)
    def _():
        greet(dev(pos + 1, other))

    def remote(src, dst, send, recv, target):
        return pltpu.make_async_remote_copy(
            src_ref=src, dst_ref=dst, send_sem=send, recv_sem=recv,
            device_id={"clus": target}, device_id_type=MESH,
        )

    def right(h, q):
        src = unit if h == 0 else from_l.at[h - 1]
        return remote(src.at[q], from_l.at[h, q], r_send.at[h, q], r_recv.at[h, q], dev(pos + 1, core))

    def left(h, q):
        src = unit if h == 0 else from_r.at[h - 1]
        c = swap(pos - 1, core) if h == reach - 1 else core
        return remote(src.at[q], from_r.at[h, q], l_send.at[h, q], l_recv.at[h, q], dev(pos - 1, c))

    def cross(h, q):
        src = unit if h == 0 else from_r.at[h - 1]
        return remote(src.at[q], across.at[h, q], x_send.at[h, q], x_recv.at[h, q], dev(pos, other))

    def normalize(q):
        step = 32
        for s in range(0, TILE, step):
            wide = emb_ref[q * TILE + s : q * TILE + s + step, :].astype(jnp.float32)
            total = jnp.sum(wide * wide, axis=1, keepdims=True)
            unit[q, s : s + step, :] = (wide * lax.rsqrt(total + 1e-06)).astype(jnp.bfloat16)

    for q in range(parts):
        loads[q].wait()
        normalize(q)
        if q == 0:
            pl.semaphore_wait(barrier, 3 + crossed(pos - 1))
        right(0, q).start()
        left(0, q).start()
        cross(0, q).start()
    for load in loads[parts:]:
        load.wait()

    def rows_of(ref, q):
        return ref[q]

    def product(x, y):
        return lax.dot_general(x, y, NT, preferred_element_type=jnp.float32)

    def top(prod, cluster):
        index = lax.broadcasted_iota(jnp.int32, prod.shape, 0)
        live = index < counts_ref[cluster]
        return jnp.max(jnp.where(live, prod, -jnp.inf), axis=0, keepdims=True)

    def block(ref):
        return ref[...].reshape(parts * TILE, width)

    self_prod = product(block(unit), block(unit))
    for t in range(parts):
        piece = self_prod[t * TILE : (t + 1) * TILE]
        table[me * parts + t] = top(piece, me * parts + t)
        square = piece[:, t * TILE : (t + 1) * TILE]
        i0 = lax.broadcasted_iota(jnp.int32, square.shape, 0)
        i1 = lax.broadcasted_iota(jnp.int32, square.shape, 1)
        count = counts_ref[me * parts + t]
        keep = (i0 < count) & (i0 != i1)
        value = jnp.max(jnp.where(keep, square, -jnp.inf), axis=0, keepdims=True)
        lane = lax.broadcasted_iota(jnp.int32, value.shape, 1)
        own_ref[t * TILE : (t + 1) * TILE] = jnp.where(lane < count, value, 0.0).reshape(TILE)

    for q in range(parts):
        cross(0, q).wait_recv()
    mate = dev(pos, other)
    mate_prod = product(block(across.at[0]), block(unit))
    for t in range(parts):
        table[mate * parts + t] = top(mate_prod[t * TILE : (t + 1) * TILE], mate * parts + t)

    def split(d):
        j = max(1, d // 2)
        return d - j, j

    def a_msg(d):
        i, j = split(d)
        if d == far:
            b = dev(pos + j, swap(pos, core))
            count = parts
        else:
            b = dev(pos + j, 0)
            count = parts * CORES
        return remote(
            res_a.at[d - 1, pl.ds(0, count)], table.at[pl.ds(b * parts, count)],
            a_send.at[d - 1], a_recv.at[d - 1], dev(pos - i, core),
        )

    def b_msg(d, e, slot):
        i, j = split(d)
        target = dev(pos + j, swap(pos, core) if d == far else e)
        a = dev(pos - i, core)
        return remote(
            res_b.at[d - 1, e], table.at[pl.ds(a * parts, parts)],
            b_send.at[d - 1, e], b_recv.at[d - 1, slot], target,
        )

    def messages(d):
        i, _ = split(d)
        found = [b_msg(d, e, 0 if d == far else core) for e in range(1 if d == far else CORES)]
        if i > 0:
            found.append(a_msg(d))
        return found

    def score(d, a_ref, b_ref, e, b_dev, a_q, b_q):
        i, _ = split(d)
        a_dev = dev(pos - i, core)
        qa, qb = a_q, b_q
        a = jnp.concatenate([a_ref[q] for q in qa], axis=0) if len(qa) > 1 else a_ref[qa[0]]
        b = jnp.concatenate([b_ref[q] for q in qb], axis=0) if len(qb) > 1 else b_ref[qb[0]]
        up = product(b, a)
        for n, t in enumerate(qb):
            value = top(up[n * TILE : (n + 1) * TILE], b_dev * parts + t)
            lanes = slice(qa[0] * TILE, (qa[-1] + 1) * TILE)
            if i == 0:
                table[b_dev * parts + t, :, lanes] = value
            else:
                slot = t if d == far else e * parts + t
                res_a[d - 1, slot, :, lanes] = value
        down = product(a, b)
        for n, t in enumerate(qa):
            value = top(down[n * TILE : (n + 1) * TILE], a_dev * parts + t)
            res_b[d - 1, 0 if d == far else e, t, :, qb[0] * TILE : (qb[-1] + 1) * TILE] = value

    every = list(range(parts))

    def near(d, a_q):
        i, j = split(d)
        a_ref = unit if i == 0 else from_l.at[i - 1]
        for mine in (True, False):
            b_ref = from_r.at[j - 1] if mine else across.at[j]
            e = core if mine else other
            score(d, a_ref, b_ref, e, dev(pos + j, e), a_q, every)

    for h in range(1, reach + 1):
        last = h == reach
        for q in range(parts):
            right(h - 1, q).wait_recv()
            if not last:
                right(h, q).start()
            left(h - 1, q).wait_recv()
            if not last:
                left(h, q).start()
                cross(h, q).start()
            if last:
                near(2 * h - 1, [q])
                if q == parts - 1:
                    for msg in messages(2 * h - 1):
                        msg.start()
                b_dev = dev(pos + reach, swap(pos, core))
                pieces = [(q, [z for z in every if z <= q])] + [(z, [q]) for z in range(q)]
                for qa, qb in pieces:
                    score(far, from_l.at[h - 1], from_r.at[h - 1], 0, b_dev, [qa], qb)
        if last:
            for msg in messages(far):
                msg.start()
        else:
            for q in range(parts):
                cross(h, q).wait_recv()
            for d in (2 * h - 1, 2 * h):
                near(d, every)
                for msg in messages(d):
                    msg.start()

    for h in range(reach):
        for q in range(parts):
            right(h, q).wait_send()
            left(h, q).wait_send()
            cross(h, q).wait_send()
    for d in range(1, far + 1):
        for msg in messages(d):
            msg.wait_send()
        for e in range(1 if d == far else CORES):
            b_msg(d, e, e).wait_recv()
        if split(d)[0] > 0:
            a_msg(d).wait_recv()

    lane = lax.broadcasted_iota(jnp.int32, (1, rows), 1)
    live = lane < 0
    for t in range(parts):
        live = live | ((lane >= t * TILE) & (lane < t * TILE + counts_ref[me * parts + t]))
    for k in range(best_ref.shape[0]):
        best_ref[k : k + 1, :] = jnp.where(live, table[wanted_ref[k]], 0.0)


def settle(best_in, own_in, best_out, own_out):
    best_out[...] = best_in[...]
    own_out[...] = own_in[...]


def body(chips, cols, emb, wanted, counts):
    rows, width = emb.shape
    parts = rows // TILE
    reach = chips // 4
    far = 2 * reach
    data = pltpu.SemaphoreType.DMA((reach, parts))
    req = wanted.shape[0]
    hbm = pl.BlockSpec(memory_space=pltpu.HBM)
    vmem = pl.BlockSpec(memory_space=pltpu.VMEM)
    best, own = pl.pallas_call(
        functools.partial(kernel, chips, cols),
        out_shape=(
            jax.ShapeDtypeStruct((req, rows), jnp.float32),
            jax.ShapeDtypeStruct((rows,), jnp.float32),
        ),
        in_specs=[hbm, hbm, hbm],
        out_specs=(vmem, vmem),
        scratch_shapes=[
            pltpu.SMEM(wanted.shape, jnp.int32),
            pltpu.SMEM(counts.shape, jnp.int32),
            pltpu.VMEM((rows, width), jnp.bfloat16),
            pltpu.SemaphoreType.DMA((parts + 2,)),
            pltpu.VMEM((parts, TILE, width), jnp.bfloat16),
            pltpu.VMEM((reach, parts, TILE, width), jnp.bfloat16),
            pltpu.VMEM((reach, parts, TILE, width), jnp.bfloat16),
            pltpu.VMEM((reach, parts, TILE, width), jnp.bfloat16),
            pltpu.VMEM((chips * CORES * parts, 1, rows), jnp.float32),
            pltpu.VMEM((far, CORES * parts, 1, rows), jnp.float32),
            pltpu.VMEM((far, CORES, parts, 1, rows), jnp.float32),
            data, data, data, data, data, data,
            pltpu.SemaphoreType.DMA((far,)),
            pltpu.SemaphoreType.DMA((far,)),
            pltpu.SemaphoreType.DMA((far, CORES)),
            pltpu.SemaphoreType.DMA((far, CORES)),
        ],
        compiler_params=pltpu.CompilerParams(collective_id=0, has_side_effects=True, vmem_limit_bytes=(3 * reach + 2) * rows * width * 2 + (8 << 20)),
    )(*(pltpu.with_memory_space_constraint(z, pltpu.HBM) for z in (wanted, counts, emb)))
    return pl.pallas_call(
        settle,
        out_shape=(
            jax.ShapeDtypeStruct(best.shape, best.dtype),
            jax.ShapeDtypeStruct(own.shape, own.dtype),
        ),
        in_specs=[vmem, vmem],
        out_specs=(vmem, vmem),
        compiler_params=pltpu.CompilerParams(vmem_limit_bytes=1 << 20),
    )(best, own)


def solution(mesh):
    chips = mesh.shape["clus"] // CORES
    cols = LAYER // mesh.shape["slab"]
    in_specs = (P(("slab", "clus"), None), P(("slab", "clus")), P("slab"))
    out_specs = (P(None, ("slab", "clus")), P(("slab", "clus")))
    return jax.shard_map(
        functools.partial(body, chips, cols), mesh=mesh,
        in_specs=in_specs, out_specs=out_specs, check_vma=False,
    )
```
